32 devices in a mesh: ctx: 8 (over z, x), wt: 4 (over y, core).
Axes of the slice: x: 2, y: 2, z: 4, core: 2. Of those that a mesh axis runs over, the one named last changes fastest.
Arguments:
- hidden_in: bfloat16 [2, 4, 1024, 960], P(None, 'wt', 'ctx'), may hold values from -6 to 6
- d_out: bfloat16 [2, 4, 1024, 960], P(None, 'wt', 'ctx'), may hold values from -6 to 6
- block_order: int32 [2, 16], replicated, may hold values from 0 to 15, as said below
- gain_attn: bfloat16 [960], P('wt'), may hold values from 0.5 to 1.5
- gain_mlp: bfloat16 [960], P('wt'), may hold values from 0.5 to 1.5
- w_q: bfloat16 [960, 960], P('wt'), may hold values from -0.25 to 0.25
- w_kv: bfloat16 [960, 640], P('wt'), may hold values from -0.1875 to 0.1875
- w_o: bfloat16 [960, 960], P('wt'), may hold values from -3 to 3
- w_gu: bfloat16 [960, 5120], P('wt'), may hold values from -0.1875 to 0.1875
- w_down: bfloat16 [2560, 960], P('wt'), may hold values from -0.25 to 0.25
Outputs:
- hidden_out: bfloat16 [2, 4, 1024, 960], P(None, 'wt', 'ctx')
- grad_in: bfloat16 [2, 4, 1024, 960], P(None, 'wt', 'ctx')
- grad_gain_attn: float32 [960], P('wt')
- grad_gain_mlp: float32 [960], P('wt')
- grad_w_q: float32 [960, 960], P('wt')
- grad_w_kv: float32 [960, 640], P('wt')
- grad_w_o: float32 [960, 960], P('wt')
- grad_w_gu: float32 [960, 5120], P('wt')
- grad_w_down: float32 [2560, 960], P('wt')
The draws below stay inside these ranges and needn't reach their ends.
Inputs may be any that keep to these rules, and one draw needn't show every extreme that they name: block_order[m] is a permutation of the 16 blocks in which stored blocks 2c and 2c + 1 are a mirrored pair: their numbers add up to 15.
All inputs are finite; a program needn't handle non-finite values.
Results may differ from the reference program's by a relative error of at most 0.018.
Values may be sent and summed in bfloat16 or wider, within the bound.
A program may use at most 256 MiB of HBM per device.

```python
import math
import jax
import jax.numpy as jnp
from jax import lax

D = 960
QH = 15
KVH = 5
HD = 64
FF = 2560
MB = 2
NBLK = 16
SEQLEN = 1024
KVD = 640
N_WT = 4


def draw_block_order(key, part):
    keys_all = jax.random.split(jax.random.fold_in(key, 17), MB)

    def one_batch(sub_key):
        pair_key, flip_key = jax.random.split(sub_key)
        pairs = jax.random.permutation(pair_key, NBLK // 2).astype(jnp.int32)
        flips = jax.random.randint(flip_key, (NBLK // 2,), 0, 2, dtype=jnp.int32)
        first_block = jnp.where(flips == 1, NBLK - 1 - pairs, pairs)
        second_block = NBLK - 1 - first_block
        return jnp.stack([first_block, second_block], axis=1).reshape(NBLK).astype(jnp.int32)
    return jax.vmap(one_batch)(keys_all)


def shard_levels(rng, dims, pieces, least, largest):
    def one(dim, shards_of):
        steps = jax.random.uniform(jax.random.fold_in(jax.random.fold_in(rng, 6), dim), (shards_of,), jnp.float32, least / len(pieces), largest / len(pieces))
        return jnp.repeat(jnp.exp(steps), dims[dim] // shards_of).reshape((-1,) + (1,) * (len(dims) - dim - 1))

    factor_of = one(*pieces[0])
    for cut in pieces[1:]:
        factor_of = factor_of * one(*cut)
    return factor_of


def centred(stream_key, extent, scale, limit, cuts=(), held_as=jnp.bfloat16):
    values = jax.random.normal(stream_key, extent, jnp.float32) * scale
    if len(cuts) > 0:
        values = shard_levels(stream_key, extent, cuts, -0.22, 0.18) * values
    return jnp.clip(values, min=-limit, max=limit).astype(held_as)


def setup_inputs(seed: int = 0) -> dict:
    splits = jax.random.split(jax.random.key(seed), 11)
    return {
        "hidden_in": centred(splits[0], (MB, N_WT, SEQLEN, D), 1.0, 6.0, ((1, 4), (2, 8))),
        "d_out": centred(splits[1], (MB, N_WT, SEQLEN, D), 1.0, 6.0, ((1, 4), (2, 8))),
        "block_order": draw_block_order(jax.random.fold_in(splits[10], 71), 0),
        "gain_attn": jnp.clip(1.0 + 0.1 * jax.random.normal(splits[3], (D,), jnp.float32), 0.5, 1.5).astype(jnp.bfloat16),
        "gain_mlp": jnp.clip(1.0 + 0.1 * jax.random.normal(splits[4], (D,), jnp.float32), 0.5, 1.5).astype(jnp.bfloat16),
        "w_q": centred(splits[5], (D, D), (D // 2) ** -0.5, 0.25, ((0, 4),)),
        "w_kv": centred(splits[6], (D, KVD), D ** -0.5, 0.1875, ((0, 4),)),
        "w_o": centred(splits[7], (D, D), (max(D // 240, 1)) ** -0.5, 3.0, ((0, 4),)),
        "w_gu": centred(splits[8], (D, 2 * FF), D ** -0.5, 0.1875, ((0, 4),)),
        "w_down": centred(splits[9], (FF, D), (FF // 4) ** -0.5, 0.25, ((0, 4),)),
    }


eps_norm = 1e-05
rope_base = 10000.0

@jax.custom_vjp
def low(v):
    return lax.optimization_barrier(v.astype(jnp.bfloat16)).astype(jnp.float32)

@jax.custom_vjp
def low_back(v):
    return v

def low_keep(v):
    return (low(v), None)

def low_pass(kept, grad):
    return (grad,)

def back_keep(v):
    return (v, None)

def back_low(kept, grad):
    return (low(grad),)
low.defvjp(low_keep, low_pass)
low_back.defvjp(back_keep, back_low)

def matmul(left, right):
    return jnp.dot(left, right, precision=lax.Precision.HIGHEST, preferred_element_type=jnp.float32)

def norm_scale(values, gain):
    return values * lax.rsqrt(lax.optimization_barrier(jnp.mean(values * values, axis=-1, keepdims=True)) + eps_norm) * gain

def rope_tables(positions):
    half_dim = HD // 2
    frequency = jnp.exp(jnp.arange(half_dim, dtype=jnp.float32) * (-2.0 * math.log(rope_base) / HD))
    angles = positions.astype(jnp.float32)[:, None] * frequency[None, :]
    return (jnp.cos(angles), jnp.sin(angles))

def rotate(values, cosine, sine):
    half_dim = values.shape[-1] // 2
    first_half = values[..., :half_dim]
    second_half = values[..., half_dim:]
    cos_wide = cosine[:, None, :]
    sin_wide = sine[:, None, :]
    return jnp.concatenate([first_half * cos_wide - second_half * sin_wide, second_half * cos_wide + first_half * sin_wide], axis=-1)

def layer(params, tokens_in, order_row):
    gain_one, gain_two, weight_q, weight_kv, weight_o, weight_gu, weight_down = params
    seq_len = tokens_in.shape[0]
    half_block = seq_len // NBLK
    positions = (order_row[:, None] * half_block + jnp.arange(half_block, dtype=jnp.int32)[None, :]).reshape(seq_len).astype(jnp.int32)
    cosine, sine = rope_tables(positions)
    act_one = low(norm_scale(tokens_in, gain_one))
    query_lin = low_back(matmul(act_one, weight_q))
    queries = low(rotate(query_lin.reshape(seq_len, QH, HD), cosine, sine))
    kv_lin = low_back(matmul(act_one, weight_kv))
    keys = low(rotate(kv_lin[:, :KVH * HD].reshape(seq_len, KVH, HD), cosine, sine))
    values = low(kv_lin[:, KVH * HD:].reshape(seq_len, KVH, HD))
    keys_all = jnp.repeat(keys, QH // KVH, axis=1)
    values_all = jnp.repeat(values, QH // KVH, axis=1)
    query_block = math.gcd(seq_len, 512)
    score_scale = 1.0 / math.sqrt(HD)

    def attend(item):
        query_part, pos_part = item
        scores = low_back(jnp.einsum('qhd,khd->hqk', query_part, keys_all, precision=lax.Precision.HIGHEST) * score_scale)
        visible = positions[None, None, :] <= pos_part[None, :, None]
        top = lax.optimization_barrier(jnp.max(jnp.where(visible, scores, -1e+30), axis=-1, keepdims=True))
        lse = top + jnp.log(lax.optimization_barrier(jnp.sum(jnp.where(visible, jnp.exp(scores - top), 0.0), axis=-1, keepdims=True)))
        probs = low(jnp.where(visible, jnp.exp(scores - lse), 0.0))
        return jnp.einsum('hqk,khd->qhd', probs, values_all, precision=lax.Precision.HIGHEST)
    attended = lax.map(jax.checkpoint(attend), (queries.reshape(seq_len // query_block, query_block, QH, HD), positions.reshape(seq_len // query_block, query_block)))
    attn = low_back(low(attended.reshape(seq_len, QH * HD)))
    mid = tokens_in + low_back(matmul(attn, weight_o))
    act_two = low(norm_scale(mid, gain_two))
    gate_up = low_back(matmul(act_two, weight_gu))
    hidden = low(jax.nn.silu(gate_up[:, :FF]) * gate_up[:, FF:])
    return mid + low_back(matmul(hidden, weight_down))

def reference(hidden_in, d_out, block_order, gain_attn, gain_mlp, w_q, w_kv, w_o, w_gu, w_down):
    params = tuple((item.astype(jnp.float32) for item in (gain_attn, gain_mlp, w_q, w_kv, w_o, w_gu, w_down)))
    tokens_all = hidden_in.astype(jnp.float32).reshape(MB * N_WT, SEQLEN, D)
    orders = jnp.repeat(block_order, N_WT, axis=0).astype(jnp.int32)

    def forward(weights, tokens):

        def one_sequence(item):
            seq_tokens, order_row = item
            return layer(weights, seq_tokens, order_row)
        return lax.map(one_sequence, (tokens, orders))
    result, pull = jax.vjp(forward, params, tokens_all)
    grad_params, grad_tokens = pull(d_out.astype(jnp.float32).reshape(MB * N_WT, SEQLEN, D))
    hidden_out = result.reshape(MB, N_WT, SEQLEN, D).astype(jnp.bfloat16)
    grad_in = grad_tokens.reshape(MB, N_WT, SEQLEN, D).astype(jnp.bfloat16)
    return (hidden_out, grad_in, grad_params[0], grad_params[1], grad_params[2], grad_params[3], grad_params[4], grad_params[5], grad_params[6])
```

```python
import math

import functools

import jax
import jax.numpy as jnp
from jax import lax
from jax.experimental import pallas as pl
from jax.experimental.pallas import tpu as pltpu
from jax.sharding import PartitionSpec as P

QH = 15
KVH = 5
HD = 64


eps_norm = 1e-05
rope_base = 10000.0


def norm_scale(values, gain):
    return values * lax.rsqrt(jnp.mean(values * values, axis=-1, keepdims=True) + eps_norm) * gain


def rope_tables(positions):
    half_dim = HD // 2
    frequency = jnp.exp(jnp.arange(half_dim, dtype=jnp.float32) * (-2.0 * math.log(rope_base) / HD))
    angles = positions.astype(jnp.float32)[:, None] * frequency[None, :]
    return (jnp.cos(angles), jnp.sin(angles))


def rotate(values, cosine, sine):
    half_dim = values.shape[-1] // 2
    first_half = values[..., :half_dim]
    second_half = values[..., half_dim:]
    cos_wide = cosine[:, None, :]
    sin_wide = sine[:, None, :]
    return jnp.concatenate(
        [
            first_half * cos_wide - second_half * sin_wide,
            second_half * cos_wide + first_half * sin_wide,
        ],
        axis=-1,
    )


def unrotate(values, cosine, sine):
    half_dim = values.shape[-1] // 2
    first_half = values[..., :half_dim]
    second_half = values[..., half_dim:]
    cos_wide = cosine[:, None, :]
    sin_wide = sine[:, None, :]
    return jnp.concatenate(
        [
            first_half * cos_wide + second_half * sin_wide,
            second_half * cos_wide - first_half * sin_wide,
        ],
        axis=-1,
    )


def block_size(total_rows, limit):
    best_size = 1
    for candidate in range(1, min(total_rows, limit) + 1):
        if total_rows % candidate == 0:
            best_size = candidate
    return best_size


def outer_sum(left, right):
    return lax.dot_general(
        left, right, (((0,), (0,)), ((), ())), preferred_element_type=jnp.float32
    )


def back_product(left, weight):
    return lax.dot_general(
        left, weight, (((1,), (1,)), ((), ())), preferred_element_type=jnp.float32
    )


def block_scores(query_groups, keys_block, key_pos, row_pos, score_scale):
    scores = (
        jnp.einsum("hrd,khd->hrk", query_groups, keys_block, preferred_element_type=jnp.float32)
        * score_scale
    )
    visible = key_pos[None, None, :] <= row_pos[None, :, None]
    return (scores, visible)


def local_general(hidden_in, d_out, block_order, gain_attn, gain_mlp, w_q, w_kv, w_o, w_gu, w_down):
    gathered = (
        lax.all_gather(gain_attn, "wt", axis=0, tiled=True),
        lax.all_gather(gain_mlp, "wt", axis=0, tiled=True),
        lax.all_gather(w_q, "wt", axis=0, tiled=True),
        lax.all_gather(w_kv, "wt", axis=0, tiled=True),
        lax.all_gather(w_o, "wt", axis=0, tiled=True),
        lax.all_gather(w_gu, "wt", axis=0, tiled=True),
        lax.all_gather(w_down, "wt", axis=0, tiled=True),
    )
    gain_one = gathered[0].astype(jnp.float32)
    gain_two = gathered[1].astype(jnp.float32)
    weight_q, weight_kv, weight_o, weight_gu, weight_down = (
        gathered[2],
        gathered[3],
        gathered[4],
        gathered[5],
        gathered[6],
    )
    micro_count = hidden_in.shape[0]
    seg_rows = hidden_in.shape[2]
    n_ctx = lax.axis_size("ctx")
    seq_len = seg_rows * n_ctx
    half_block = seg_rows // 2
    kv_width = KVH * HD
    group_size = QH // KVH
    row_count = group_size * seg_rows
    ff_width = weight_down.shape[0]
    key_block = block_size(seq_len, 1024)
    block_count = seq_len // key_block
    score_scale = 1.0 / math.sqrt(HD)
    my_start = lax.axis_index("ctx") * seg_rows
    grad_names = [jnp.zeros(item.shape, jnp.float32) for item in gathered]
    outputs = []
    input_grads = []
    for micro_index in range(micro_count):
        tokens_in = hidden_in[micro_index, 0].astype(jnp.float32)
        order_row = block_order[micro_index]
        key_pos = (
            order_row[:, None] * half_block + jnp.arange(half_block, dtype=jnp.int32)[None, :]
        ).reshape(seq_len)
        query_pos = lax.dynamic_slice_in_dim(key_pos, my_start, seg_rows)
        row_pos = jnp.tile(query_pos, group_size)
        cosine, sine = rope_tables(query_pos)
        normed_one, pull_one = jax.vjp(norm_scale, tokens_in, gain_one)
        act_one = normed_one.astype(jnp.bfloat16)
        query_lin = jnp.dot(act_one, weight_q, preferred_element_type=jnp.float32).reshape(
            seg_rows, QH, HD
        )
        query_rot = rotate(query_lin, cosine, sine).astype(jnp.bfloat16)
        query_groups = (
            query_rot.reshape(seg_rows, KVH, group_size, HD)
            .transpose(1, 2, 0, 3)
            .reshape(KVH, row_count, HD)
        )
        kv_lin = jnp.dot(act_one, weight_kv, preferred_element_type=jnp.float32)
        key_rot = rotate(kv_lin[:, :kv_width].reshape(seg_rows, KVH, HD), cosine, sine).reshape(
            seg_rows, kv_width
        )
        kv_send = jnp.concatenate([key_rot, kv_lin[:, kv_width:]], axis=1).astype(jnp.bfloat16)
        kv_whole = lax.all_gather(kv_send, "ctx", axis=0, tiled=True)
        kv_blocks = kv_whole.reshape(block_count, key_block, 2 * kv_width)
        pos_blocks = key_pos.reshape(block_count, key_block)

        def lse_step(carry, item):
            top_now, total_now = carry
            kv_block, kpos = item
            keys_block = kv_block[:, :kv_width].reshape(key_block, KVH, HD)
            scores, visible = block_scores(query_groups, keys_block, kpos, row_pos, score_scale)
            top_new = jnp.maximum(top_now, jnp.max(jnp.where(visible, scores, -1e30), axis=-1))
            total_new = total_now * jnp.exp(top_now - top_new) + jnp.sum(
                jnp.where(visible, jnp.exp(scores - top_new[..., None]), 0.0), axis=-1
            )
            return ((top_new, total_new), None)

        start_top = jnp.full((KVH, row_count), -1e30, jnp.float32)
        start_total = jnp.zeros((KVH, row_count), jnp.float32)
        (top_all, total_all), _ = lax.scan(
            lse_step, (start_top, start_total), (kv_blocks, pos_blocks)
        )
        lse = top_all + jnp.log(total_all)

        def value_step(acc_now, item):
            kv_block, kpos = item
            keys_block = kv_block[:, :kv_width].reshape(key_block, KVH, HD)
            vals_block = kv_block[:, kv_width:].reshape(key_block, KVH, HD)
            scores, visible = block_scores(query_groups, keys_block, kpos, row_pos, score_scale)
            probs = jnp.where(visible, jnp.exp(scores - lse[..., None]), 0.0).astype(jnp.bfloat16)
            return (
                acc_now
                + jnp.einsum("hrk,khd->hrd", probs, vals_block, preferred_element_type=jnp.float32),
                None,
            )

        acc_all, _ = lax.scan(
            value_step, jnp.zeros((KVH, row_count, HD), jnp.float32), (kv_blocks, pos_blocks)
        )
        attn_low = (
            acc_all.reshape(KVH, group_size, seg_rows, HD)
            .transpose(2, 0, 1, 3)
            .reshape(seg_rows, QH * HD)
            .astype(jnp.bfloat16)
        )
        mid_state = tokens_in + jnp.dot(attn_low, weight_o, preferred_element_type=jnp.float32)
        normed_two, pull_two = jax.vjp(norm_scale, mid_state, gain_two)
        act_two = normed_two.astype(jnp.bfloat16)
        gate_up = jnp.dot(act_two, weight_gu, preferred_element_type=jnp.float32)
        gate_part = gate_up[:, :ff_width]
        up_part = gate_up[:, ff_width:]
        sig_gate = jax.nn.sigmoid(gate_part)
        hidden_low = (gate_part * sig_gate * up_part).astype(jnp.bfloat16)
        result = mid_state + jnp.dot(hidden_low, weight_down, preferred_element_type=jnp.float32)
        outputs.append(result.astype(jnp.bfloat16))
        grad_low = d_out[micro_index, 0]
        grad_top = grad_low.astype(jnp.float32)
        grad_down = outer_sum(hidden_low, grad_low)
        d_hidden = back_product(grad_low, weight_down)
        d_gate = d_hidden * up_part * sig_gate * (1.0 + gate_part * (1.0 - sig_gate))
        d_up = d_hidden * gate_part * sig_gate
        d_gu_low = jnp.concatenate([d_gate, d_up], axis=1).astype(jnp.bfloat16)
        grad_gu = outer_sum(act_two, d_gu_low)
        d_act_two = back_product(d_gu_low, weight_gu)
        d_mid_norm, grad_gain_two = pull_two(d_act_two)
        d_mid = grad_top + d_mid_norm
        d_mid_low = d_mid.astype(jnp.bfloat16)
        grad_o = outer_sum(attn_low, d_mid_low)
        d_attn_low = back_product(d_mid_low, weight_o).astype(jnp.bfloat16)
        grad_groups = (
            d_attn_low.reshape(seg_rows, KVH, group_size, HD)
            .transpose(1, 2, 0, 3)
            .reshape(KVH, row_count, HD)
        )
        kv_back = lax.all_gather(kv_send, "ctx", axis=0, tiled=True).reshape(
            block_count, key_block, 2 * kv_width
        )

        def delta_step(delta_now, item):
            kv_block, kpos = item
            keys_block = kv_block[:, :kv_width].reshape(key_block, KVH, HD)
            vals_block = kv_block[:, kv_width:].reshape(key_block, KVH, HD)
            scores, visible = block_scores(query_groups, keys_block, kpos, row_pos, score_scale)
            probs = jnp.where(visible, jnp.exp(scores - lse[..., None]), 0.0)
            d_probs = jnp.einsum(
                "hrd,khd->hrk", grad_groups, vals_block, preferred_element_type=jnp.float32
            )
            return (delta_now + jnp.sum(probs * d_probs, axis=-1), None)

        delta, _ = lax.scan(
            delta_step, jnp.zeros((KVH, row_count), jnp.float32), (kv_back, pos_blocks)
        )

        def grad_step(dq_now, item):
            kv_block, kpos = item
            keys_block = kv_block[:, :kv_width].reshape(key_block, KVH, HD)
            vals_block = kv_block[:, kv_width:].reshape(key_block, KVH, HD)
            scores, visible = block_scores(query_groups, keys_block, kpos, row_pos, score_scale)
            probs = jnp.where(visible, jnp.exp(scores - lse[..., None]), 0.0)
            d_probs = jnp.einsum(
                "hrd,khd->hrk", grad_groups, vals_block, preferred_element_type=jnp.float32
            )
            d_scores = (probs * (d_probs - delta[..., None])).astype(jnp.bfloat16)
            dq_new = dq_now + jnp.einsum(
                "hrk,khd->hrd", d_scores, keys_block, preferred_element_type=jnp.float32
            )
            d_keys = (
                jnp.einsum(
                    "hrk,hrd->khd", d_scores, query_groups, preferred_element_type=jnp.float32
                )
                * score_scale
            )
            d_vals = jnp.einsum(
                "hrk,hrd->khd",
                probs.astype(jnp.bfloat16),
                grad_groups,
                preferred_element_type=jnp.float32,
            )
            return (
                dq_new,
                jnp.concatenate(
                    [d_keys.reshape(key_block, kv_width), d_vals.reshape(key_block, kv_width)],
                    axis=1,
                ),
            )

        dq_groups, dkv_blocks = lax.scan(
            grad_step, jnp.zeros((KVH, row_count, HD), jnp.float32), (kv_back, pos_blocks)
        )
        dkv_mine = lax.psum_scatter(
            dkv_blocks.reshape(seq_len, 2 * kv_width), "ctx", scatter_dimension=0, tiled=True
        )
        d_query = (
            (dq_groups * score_scale)
            .reshape(KVH, group_size, seg_rows, HD)
            .transpose(2, 0, 1, 3)
            .reshape(seg_rows, QH, HD)
        )
        d_q_low = unrotate(d_query, cosine, sine).reshape(seg_rows, QH * HD).astype(jnp.bfloat16)
        d_key = unrotate(dkv_mine[:, :kv_width].reshape(seg_rows, KVH, HD), cosine, sine).reshape(
            seg_rows, kv_width
        )
        d_kv_low = jnp.concatenate([d_key, dkv_mine[:, kv_width:]], axis=1).astype(jnp.bfloat16)
        grad_q = outer_sum(act_one, d_q_low)
        grad_kv = outer_sum(act_one, d_kv_low)
        d_act_one = back_product(d_q_low, weight_q) + back_product(d_kv_low, weight_kv)
        d_in_norm, grad_gain_one = pull_one(d_act_one)
        input_grads.append((d_mid + d_in_norm).astype(jnp.bfloat16))
        parts_now = [grad_gain_one, grad_gain_two, grad_q, grad_kv, grad_o, grad_gu, grad_down]
        grad_names = [total + piece for total, piece in zip(grad_names, parts_now)]
    owned = (
        lax.psum_scatter(
            grad_names[0].astype(jnp.bfloat16), "wt", scatter_dimension=0, tiled=True
        ).astype(jnp.float32),
        lax.psum_scatter(
            grad_names[1].astype(jnp.bfloat16), "wt", scatter_dimension=0, tiled=True
        ).astype(jnp.float32),
        lax.psum_scatter(
            grad_names[2].astype(jnp.bfloat16), "wt", scatter_dimension=0, tiled=True
        ).astype(jnp.float32),
        lax.psum_scatter(
            grad_names[3].astype(jnp.bfloat16), "wt", scatter_dimension=0, tiled=True
        ).astype(jnp.float32),
        lax.psum_scatter(
            grad_names[4].astype(jnp.bfloat16), "wt", scatter_dimension=0, tiled=True
        ).astype(jnp.float32),
        lax.psum_scatter(
            grad_names[5].astype(jnp.bfloat16), "wt", scatter_dimension=0, tiled=True
        ).astype(jnp.float32),
        lax.psum_scatter(
            grad_names[6].astype(jnp.bfloat16), "wt", scatter_dimension=0, tiled=True
        ).astype(jnp.float32),
    )
    summed = lax.psum((owned[0], owned[1], owned[2], owned[3], owned[4], owned[5], owned[6]), "ctx")
    hidden_out = jnp.stack(outputs)[:, None]
    grad_in = jnp.stack(input_grads)[:, None]
    return (
        hidden_out,
        grad_in,
        summed[0],
        summed[1],
        summed[2],
        summed[3],
        summed[4],
        summed[5],
        summed[6],
    )


MESH = pl.DeviceIdType.MESH
ANY = pl.BlockSpec(memory_space=pl.ANY)
VMEM = pl.BlockSpec(memory_space=pltpu.VMEM)
BF = jnp.bfloat16
F32 = jnp.float32


class Place:
    def __init__(self):
        ctx = lax.axis_index("ctx")
        wt = lax.axis_index("wt")
        self.ctx, self.wt = ctx, wt
        self.z, self.x = ctx // 2, ctx % 2
        self.y, self.c = wt // 2, wt % 2

    def dev(self, z=None, x=None, y=None, c=None):
        z = self.z if z is None else z
        x = self.x if x is None else x
        y = self.y if y is None else y
        c = self.c if c is None else c
        return {"ctx": z * 2 + x, "wt": y * 2 + c}


def barrier(devices):
    sem = pltpu.get_barrier_semaphore()
    for device in devices:
        pl.semaphore_signal(sem, inc=1, device_id=device, device_id_type=MESH)
    pl.semaphore_wait(sem, len(devices))


class Copies:
    def __init__(self, send, recv, local=None):
        self.send, self.recv, self.local = send, recv, local
        self.used = 0
        self.used_local = 0

    def remote(self, src, dst, device):
        index = self.used
        self.used += 1
        return pltpu.make_async_remote_copy(
            src_ref=src,
            dst_ref=dst,
            send_sem=self.send.at[index],
            recv_sem=self.recv.at[index],
            device_id=device,
            device_id_type=MESH,
        )

    def near(self, src, dst):
        index = self.used_local
        self.used_local += 1
        return pltpu.make_async_copy(src, dst, self.local.at[index])


def rows_of(index, size):
    return pl.ds(pl.multiple_of(index * size, size), size)


class Gather:
    def __init__(self, copies, place, axis, src, ref):
        me = getattr(place, axis)
        own = me * 2 + place.c
        across = (1 - me) * 2 + place.c
        self.place = place
        partner = place.dev(c=1 - place.c)
        self.far = copies.remote(src, ref.at[own], place.dev(**{axis: 1 - me}))
        self.near = copies.remote(src, ref.at[own], partner)
        self.relay = copies.remote(ref.at[across], ref.at[across], partner)
        self.far.start()
        self.near.start()

    def pass_on(self):
        self.far.wait_recv()
        self.relay.start()

    def wait(self):
        self.near.wait_recv()
        self.relay.wait_recv()
        self.far.wait_send()
        self.near.wait_send()
        self.relay.wait_send()


def start_kernel(hid, dout, wq, wkv, wo, wgu, gains, xs, dos, wq_o, wkv_o, wo_o, wgu_o, gains_o, send, recv, local, zsend, zrecv, zlocal):
    at = Place()
    z, x, y, c = at.z, at.x, at.y, at.c
    partners = [at.dev(c=1 - c), at.dev(y=1 - y), at.dev(y=1 - y, c=1 - c)]
    for step in (1, 2, 3):
        for core in (0, 1):
            partners.append(at.dev(z=(z + step) % 4, c=core))
    barrier(partners)
    copies = Copies(send, recv, local)
    own = at.wt

    def move(source, target, base):
        for micro in range(2):
            to_z = 2 * micro + c
            core = z // 2
            here = (to_z == z) & (core == c)
            slot = z % 2

            @pl.when(here)
            def _():
                pltpu.make_async_copy(source.at[micro, 0], target(c, slot), zlocal.at[base]).start()

            @pl.when(jnp.logical_not(here))
            def _():
                pltpu.make_async_remote_copy(
                    src_ref=source.at[micro, 0],
                    dst_ref=target(core, slot),
                    send_sem=zsend.at[base * 2 + micro],
                    recv_sem=zrecv.at[base * 2 + slot],
                    device_id=at.dev(z=to_z, c=core),
                    device_id_type=MESH,
                ).start()

    def move_wait(source, target, base):
        for micro in range(2):
            here = (2 * micro + c == z) & (z // 2 == c)

            @pl.when(jnp.logical_not(here))
            def _():
                pltpu.make_async_remote_copy(
                    src_ref=source.at[micro, 0],
                    dst_ref=target(c, 0),
                    send_sem=zsend.at[base * 2 + micro],
                    recv_sem=zrecv.at[base * 2],
                    device_id=at.dev(c=1 - c),
                    device_id_type=MESH,
                ).wait_send()

        for slot in range(2):
            here = (2 * c + slot == z) & (z % 2 == c)

            @pl.when(here)
            def _():
                pltpu.make_async_copy(source.at[0, 0], target(c, slot), zlocal.at[base]).wait()

            @pl.when(jnp.logical_not(here))
            def _():
                pltpu.make_async_remote_copy(
                    src_ref=source.at[0, 0],
                    dst_ref=target(c, slot),
                    send_sem=zsend.at[base * 2],
                    recv_sem=zrecv.at[base * 2 + slot],
                    device_id=at.dev(c=1 - c),
                    device_id_type=MESH,
                ).wait_recv()

    move(hid, lambda core, slot: xs.at[slot], 0)
    move(dout, lambda core, slot: dos.at[y * 2 + core, slot], 1)
    gathers = []
    locals_ = []
    for src, dst in ((gains, gains_o), (wq, wq_o), (wkv, wkv_o), (wo, wo_o)):
        gathers.append(Gather(copies, at, "y", src, dst))
        mine = copies.near(src, dst.at[own])
        mine.start()
        locals_.append(mine)
    columns = []
    for part in range(2):
        for y_to, c_to in ((1 - y, c), (1 - y, 1 - c), (y, 1 - c)):
            to = y_to * 2 + c_to
            copy = copies.remote(
                wgu.at[:, rows_of(part * 4 + to, 640)],
                wgu_o.at[own, :, pl.ds(part * 640, 640)],
                at.dev(y=y_to, c=c_to),
            )
            copy.start()
            columns.append(copy)
        mine = copies.near(wgu.at[:, rows_of(part * 4 + own, 640)], wgu_o.at[own, :, pl.ds(part * 640, 640)])
        mine.start()
        locals_.append(mine)
    move_wait(hid, lambda core, slot: xs.at[slot], 0)
    for gather in gathers:
        gather.pass_on()
    move_wait(dout, lambda core, slot: dos.at[y * 2 + core, slot], 1)
    gathers.append(Gather(copies, at, "y", dos.at[own], dos))
    gathers[-1].pass_on()
    for gather in gathers:
        gather.wait()
    for copy in columns:
        copy.wait_recv()
        copy.wait_send()
    for copy in locals_:
        copy.wait()


def gather_kernel(axis, src, out, send, recv, local):
    at = Place()
    me = getattr(at, axis)
    barrier([at.dev(c=1 - at.c), at.dev(**{axis: 1 - me})])
    copies = Copies(send, recv, local)
    gather = Gather(copies, at, axis, src, out)
    mine = copies.near(src, out.at[me * 2 + at.c])
    mine.start()
    gather.pass_on()
    gather.wait()
    mine.wait()


def gather_call(axis, src, collective):
    return pl.pallas_call(
        functools.partial(gather_kernel, axis),
        out_shape=jax.ShapeDtypeStruct((4,) + src.shape, src.dtype),
        in_specs=[VMEM],
        out_specs=VMEM,
        scratch_shapes=[
            pltpu.SemaphoreType.DMA((3,)),
            pltpu.SemaphoreType.DMA((3,)),
            pltpu.SemaphoreType.DMA((1,)),
        ],
        compiler_params=pltpu.CompilerParams(collective_id=collective, has_side_effects=True),
    )(src)


class Scatter:
    def __init__(self, copies, place, axis, part, one, two, three, total):
        me = getattr(place, axis)
        c = place.c
        self.me, self.c, self.part = me, c, part
        self.one, self.two, self.three, self.total = one, two, three, total
        partner = place.dev(c=1 - c)
        self.first = copies.remote(part.at[(1 - me) * 2 + 1 - c], one, partner)
        self.second = copies.remote(part.at[me * 2 + 1 - c], two, partner)
        self.across = copies.remote(total, three, place.dev(**{axis: 1 - me}))

    def start(self):
        self.first.start()
        self.second.start()

    def middle(self):
        self.first.wait_recv()
        mine = self.part[(1 - self.me) * 2 + self.c].astype(F32)
        self.total[...] = (mine + self.one[...].astype(F32)).astype(self.total.dtype)
        self.across.start()

    def finish(self):
        self.second.wait_recv()
        self.across.wait_recv()
        mine = self.part[self.me * 2 + self.c].astype(F32)
        value = mine + self.two[...].astype(F32) + self.three[...].astype(F32)
        self.first.wait_send()
        self.second.wait_send()
        self.across.wait_send()
        return value


def scatter_kernel(axis, count, *refs):
    parts, outs = refs[:count], refs[count : 2 * count]
    slots = refs[2 * count : 6 * count]
    send, recv = refs[6 * count :]
    at = Place()
    me = getattr(at, axis)
    barrier([at.dev(c=1 - at.c), at.dev(**{axis: 1 - me})])
    copies = Copies(send, recv)
    scatters = [Scatter(copies, at, axis, parts[i], *slots[4 * i : 4 * i + 4]) for i in range(count)]
    for item in scatters:
        item.start()
    for item in scatters:
        item.middle()
    for item, out in zip(scatters, outs):
        out[...] = item.finish()


def scatter_call(axis, parts, collective):
    shapes = [part.shape[1:] for part in parts]
    slots = []
    for shape in shapes:
        slots += [pltpu.VMEM(shape, BF)] * 4
    return pl.pallas_call(
        functools.partial(scatter_kernel, axis, len(parts)),
        out_shape=[jax.ShapeDtypeStruct(shape, F32) for shape in shapes],
        in_specs=[VMEM] * len(parts),
        out_specs=[VMEM] * len(parts),
        scratch_shapes=slots
        + [
            pltpu.SemaphoreType.DMA((3 * len(parts),)),
            pltpu.SemaphoreType.DMA((3 * len(parts),)),
        ],
        compiler_params=pltpu.CompilerParams(collective_id=collective, has_side_effects=True),
    )(*parts)


class Halving:
    def __init__(self, copies, place, src, dim, slots, sums, piece):
        self.copies, self.place, self.src, self.dim = copies, place, src, dim
        self.slots, self.sums, self.piece = slots, sums, piece
        z = place.z
        self.bits = (place.x, z % 2, z // 2)
        self.partners = (
            place.dev(x=1 - place.x),
            place.dev(z=z + 1 - 2 * (z % 2)),
            place.dev(z=z + 2 - 4 * (z // 2)),
        )
        self.size = src.shape[dim]
        self.pending = None

    def view(self, ref, index, size):
        if self.dim == 0:
            return ref.at[rows_of(index, size)]
        return ref.at[:, rows_of(index, size)]

    def source(self, stage):
        return self.src if stage == 0 else self.sums[stage - 1]

    def send(self, stage):
        size = self.size >> (stage + 1)
        self.pending = self.copies.remote(
            self.view(self.source(stage), 1 - self.bits[stage], size), self.slots[stage], self.partners[stage]
        )
        self.pending.start()

    def add(self, stage):
        size = self.size >> (stage + 1)
        self.pending.wait_recv()
        mine = self.view(self.source(stage), self.bits[stage], size)[...].astype(F32)
        target = self.piece if stage == 2 else self.sums[stage]
        target[...] = (mine + self.slots[stage][...].astype(F32)).astype(BF)
        self.pending.wait_send()


class Doubling:
    def __init__(self, copies, place, out, dim):
        self.copies, self.place, self.out, self.dim = copies, place, out, dim
        z = place.z
        self.index = place.x * 4 + (z % 2) * 2 + z // 2
        self.partners = (
            place.dev(x=1 - place.x),
            place.dev(z=z + 1 - 2 * (z % 2)),
            place.dev(z=z + 2 - 4 * (z // 2)),
        )
        self.size = out.shape[dim]

    def view(self, index, size):
        if self.dim == 0:
            return self.out.at[rows_of(index, size)]
        return self.out.at[:, rows_of(index, size)]

    def send(self, stage):
        size = self.size >> (stage + 1)
        index = self.index // (1 << (2 - stage))
        view = self.view(index, size)
        self.pending = self.copies.remote(view, view, self.partners[stage])
        self.pending.start()

    def wait(self):
        self.pending.wait_recv()
        self.pending.wait_send()


def end_kernel(
    qkvo, gu, down, ho, gi,
    down_o, gu_o, qkvo_o, ho_o, gi_o,
    w1, w2, w3, w4, qkvo_own,
    d1, d2, d3, ds1, ds2, g1, g2, g3, gs1, gs2, gp, q1, q2, q3, qs1, qs2,
    send, recv, local, zsend, zrecv, zlocal,
):
    at = Place()
    z, x, y, c = at.z, at.x, at.y, at.c
    partners = [
        at.dev(c=1 - c), at.dev(y=1 - y), at.dev(y=1 - y, c=1 - c), at.dev(x=1 - x),
    ]
    for step in (1, 2, 3):
        for core in (0, 1):
            partners.append(at.dev(z=(z + step) % 4, c=core))
    barrier(partners)
    copies = Copies(send, recv, local)

    def back(source, target, base):
        for slot in range(2):
            to_z = 2 * c + slot
            core = z % 2
            here = (to_z == z) & (core == c)
            micro = z // 2

            @pl.when(here)
            def _():
                pltpu.make_async_copy(source.at[slot], target.at[micro, 0], zlocal.at[base]).start()

            @pl.when(jnp.logical_not(here))
            def _():
                pltpu.make_async_remote_copy(
                    src_ref=source.at[slot],
                    dst_ref=target.at[micro, 0],
                    send_sem=zsend.at[base * 2 + slot],
                    recv_sem=zrecv.at[base * 2 + micro],
                    device_id=at.dev(z=to_z, c=core),
                    device_id_type=MESH,
                ).start()

    def back_wait(source, target, base):
        for slot in range(2):
            here = (2 * c + slot == z) & (z % 2 == c)

            @pl.when(jnp.logical_not(here))
            def _():
                pltpu.make_async_remote_copy(
                    src_ref=source.at[slot],
                    dst_ref=target.at[0, 0],
                    send_sem=zsend.at[base * 2 + slot],
                    recv_sem=zrecv.at[base * 2],
                    device_id=at.dev(c=1 - c),
                    device_id_type=MESH,
                ).wait_send()

        for micro in range(2):
            here = (2 * micro + c == z) & (z // 2 == c)

            @pl.when(here)
            def _():
                pltpu.make_async_copy(source.at[0], target.at[micro, 0], zlocal.at[base]).wait()

            @pl.when(jnp.logical_not(here))
            def _():
                pltpu.make_async_remote_copy(
                    src_ref=source.at[0],
                    dst_ref=target.at[micro, 0],
                    send_sem=zsend.at[base * 2],
                    recv_sem=zrecv.at[base * 2 + micro],
                    device_id=at.dev(c=1 - c),
                    device_id_type=MESH,
                ).wait_recv()

    scatter = Scatter(copies, at, "y", qkvo, w1, w2, w3, w4)
    scatter.start()
    index = x * 4 + (z % 2) * 2 + z // 2
    halves = [
        Halving(copies, at, down, 0, (d1, d2, d3), (ds1, ds2), down_o.at[rows_of(index, 80)]),
        Halving(copies, at, gu, 1, (g1, g2, g3), (gs1, gs2), gp),
    ]
    for half in halves:
        half.send(0)
    back(ho, ho_o, 0)
    back(gi, gi_o, 1)
    scatter.middle()
    for stage in range(3):
        for half in halves:
            half.add(stage)
            if stage < 2:
                half.send(stage + 1)
    own = at.wt
    down_back = Doubling(copies, at, down_o, 0)
    down_back.send(2)
    moved = []
    for y_to, c_to in ((1 - y, c), (1 - y, 1 - c), (y, 1 - c)):
        to = y_to * 2 + c_to
        for part in range(2):
            copy = copies.remote(
                gp.at[to, :, pl.ds(part * 640, 640)],
                gu_o.at[rows_of(index, 32), rows_of(part * 4 + own, 640)],
                at.dev(y=y_to, c=c_to),
            )
            copy.start()
            moved.append(copy)
    for part in range(2):
        gu_o[rows_of(index, 32), rows_of(part * 4 + own, 640)] = gp[own, :, part * 640 : part * 640 + 640]
    qkvo_own[...] = scatter.finish().astype(BF)
    third = Halving(copies, at, qkvo_own, 0, (q1, q2, q3), (qs1, qs2), qkvo_o.at[rows_of(index, 32)])
    third.send(0)
    down_back.wait()
    down_back.send(1)
    for copy in moved:
        copy.wait_recv()
        copy.wait_send()
    gu_back = Doubling(copies, at, gu_o, 0)
    gu_back.send(2)
    third.add(0)
    third.send(1)
    down_back.wait()
    down_back.send(0)
    gu_back.wait()
    gu_back.send(1)
    third.add(1)
    third.send(2)
    third.add(2)
    last = Doubling(copies, at, qkvo_o, 0)
    last.send(2)
    gu_back.wait()
    gu_back.send(0)
    last.wait()
    last.send(1)
    last.wait()
    last.send(0)
    down_back.wait()
    gu_back.wait()
    last.wait()
    back_wait(ho, ho_o, 0)
    back_wait(gi, gi_o, 1)


def start_call(hid, dout, wq, wkv, wo, wgu, gains):
    def out(shape):
        return jax.ShapeDtypeStruct(shape, BF)

    return pl.pallas_call(
        start_kernel,
        out_shape=[
            out((2,) + hid.shape[2:]),
            out((4, 2) + hid.shape[2:]),
            out((4,) + wq.shape),
            out((4,) + wkv.shape),
            out((4,) + wo.shape),
            out((4, wgu.shape[0], wgu.shape[1] // 4)),
            out((4,) + gains.shape),
        ],
        in_specs=[ANY] * 7,
        out_specs=[ANY] * 7,
        scratch_shapes=[
            pltpu.SemaphoreType.DMA((21,)),
            pltpu.SemaphoreType.DMA((21,)),
            pltpu.SemaphoreType.DMA((6,)),
            pltpu.SemaphoreType.DMA((4,)),
            pltpu.SemaphoreType.DMA((4,)),
            pltpu.SemaphoreType.DMA((2,)),
        ],
        compiler_params=pltpu.CompilerParams(collective_id=0, has_side_effects=True),
    )(hid, dout, wq, wkv, wo, wgu, gains)


def end_call(qkvo, gu, down, ho, gi):
    def out(shape):
        return jax.ShapeDtypeStruct(shape, BF)

    def buf(*shape):
        return pltpu.VMEM(shape, BF)

    micro = (2, 1) + ho.shape[1:]
    return pl.pallas_call(
        end_kernel,
        out_shape=[out((640, 960)), out((256, 5120)), out((256, 2560)), out(micro), out(micro)],
        in_specs=[VMEM] * 5,
        out_specs=[VMEM] * 5,
        scratch_shapes=[buf(256, 2560)] * 5
        + [buf(320, 960), buf(160, 960), buf(80, 960), buf(320, 960), buf(160, 960)]
        + [buf(4, 128, 1280), buf(4, 64, 1280), buf(4, 32, 1280), buf(4, 128, 1280), buf(4, 64, 1280), buf(4, 32, 1280)]
        + [buf(128, 2560), buf(64, 2560), buf(32, 2560), buf(128, 2560), buf(64, 2560)]
        + [
            pltpu.SemaphoreType.DMA((40,)),
            pltpu.SemaphoreType.DMA((40,)),
            pltpu.SemaphoreType.DMA((2,)),
            pltpu.SemaphoreType.DMA((4,)),
            pltpu.SemaphoreType.DMA((4,)),
            pltpu.SemaphoreType.DMA((2,)),
        ],
        compiler_params=pltpu.CompilerParams(
            collective_id=6, has_side_effects=True, vmem_limit_bytes=60 * 1024 * 1024
        ),
    )(qkvo, gu, down, ho, gi)


def local_fast(hidden_in, d_out, block_order, gain_attn, gain_mlp, w_q, w_kv, w_o, w_gu, w_down):
    at = Place()
    seg = hidden_in.shape[2]
    width = hidden_in.shape[3]
    half_block = seg // 2
    rows = 2 * seg
    kv_width = KVH * HD
    group_size = QH // KVH
    score_scale = 1.0 / math.sqrt(HD)
    gains = jnp.zeros((16, 256), BF).at[0, :240].set(gain_attn).at[1, :240].set(gain_mlp)
    xs, dos, wq, wkv, wo, wgu, gains_all = start_call(hidden_in, d_out, w_q, w_kv, w_o, w_gu, gains)
    gain_one = gains_all[:, 0, :240].reshape(width).astype(F32)
    gain_two = gains_all[:, 1, :240].reshape(width).astype(F32)
    wq = wq.reshape(width, width)
    wkv = wkv.reshape(width, 2 * kv_width)
    wo = wo.reshape(width, width)
    wgu = wgu.reshape(width, -1)
    dos = dos.reshape(4 * rows, width)

    order = lax.dynamic_index_in_dim(block_order, at.z // 2, 0, keepdims=False).reshape(4, 2, 2)
    key_pos = (
        order.transpose(1, 0, 2)[..., None] * half_block + jnp.arange(half_block, dtype=jnp.int32)
    ).reshape(4 * rows)
    row_pos = lax.dynamic_slice_in_dim(key_pos, (at.x * 2 + at.c) * rows, rows)
    cosine, sine = rope_tables(row_pos)

    tokens = xs.reshape(rows, width).astype(F32)
    normed_one, pull_one = jax.vjp(norm_scale, tokens, gain_one)
    act_one = normed_one.astype(BF)
    query = jnp.dot(act_one, wq, preferred_element_type=F32).reshape(rows, QH, HD)
    query = rotate(query, cosine, sine).astype(BF)
    query = query.reshape(rows, KVH, group_size, HD).transpose(1, 2, 0, 3)
    kv_lin = jnp.dot(act_one, wkv, preferred_element_type=F32)
    key_rot = rotate(kv_lin[:, :kv_width].reshape(rows, KVH, HD), cosine, sine).reshape(rows, kv_width)
    kv_mine = jnp.concatenate([key_rot, kv_lin[:, kv_width:]], axis=1).astype(BF)
    kv_all = gather_call("x", kv_mine, 1).reshape(4 * rows, 2 * kv_width)
    keys = kv_all[:, :kv_width].reshape(4 * rows, KVH, HD)
    vals = kv_all[:, kv_width:].reshape(4 * rows, KVH, HD)
    visible = key_pos[None, :] <= row_pos[:, None]

    scores = jnp.einsum("grqd,kgd->grqk", query, keys, preferred_element_type=F32) * score_scale
    scores = jnp.where(visible, scores, -1e30)
    top = jnp.max(scores, axis=-1, keepdims=True)
    probs = jnp.where(visible, jnp.exp(scores - top), 0.0)
    probs = probs / jnp.sum(probs, axis=-1, keepdims=True)
    attn = jnp.einsum("grqk,kgd->qgrd", probs.astype(BF), vals, preferred_element_type=F32)
    attn = attn.reshape(rows, QH * HD).astype(BF)
    mid = tokens + jnp.dot(attn, wo, preferred_element_type=F32)
    normed_two, pull_two = jax.vjp(norm_scale, mid, gain_two)
    act_two = gather_call("y", normed_two.astype(BF), 2).reshape(4 * rows, width)

    gate_up = jnp.dot(act_two, wgu, preferred_element_type=F32)
    ff = gate_up.shape[1] // 2
    gate, up = gate_up[:, :ff], gate_up[:, ff:]
    sig = jax.nn.sigmoid(gate)
    hidden = (gate * sig * up).astype(BF)
    out_part = jnp.dot(hidden, w_down, preferred_element_type=F32).astype(BF)
    grad_down = outer_sum(hidden, dos)
    d_hidden = back_product(dos, w_down)
    d_gate = d_hidden * up * sig * (1.0 + gate * (1.0 - sig))
    d_up = d_hidden * gate * sig
    d_gu = jnp.concatenate([d_gate, d_up], axis=1).astype(BF)
    grad_gu = outer_sum(act_two, d_gu)
    d_part = back_product(d_gu, wgu).astype(BF)
    out_sum, d_act_two = scatter_call(
        "y", [out_part.reshape(4, rows, width), d_part.reshape(4, rows, width)], 3
    )
    result = (mid + out_sum).astype(BF)
    d_mid_norm, grad_gain_two = pull_two(d_act_two)
    d_own = lax.dynamic_slice_in_dim(dos, at.wt * rows, rows).astype(F32)
    d_mid = d_own + d_mid_norm
    d_mid_low = d_mid.astype(BF)
    grad_o = outer_sum(attn, d_mid_low)
    d_attn = back_product(d_mid_low, wo).astype(BF)
    d_attn = d_attn.reshape(rows, KVH, group_size, HD).transpose(1, 2, 0, 3)
    d_probs = jnp.einsum("grqd,kgd->grqk", d_attn, vals, preferred_element_type=F32)
    delta = jnp.sum(probs * d_probs, axis=-1, keepdims=True)
    d_scores = (probs * (d_probs - delta)).astype(BF)
    d_query = jnp.einsum("grqk,kgd->qgrd", d_scores, keys, preferred_element_type=F32) * score_scale
    d_keys = jnp.einsum("grqk,grqd->kgd", d_scores, query, preferred_element_type=F32) * score_scale
    d_vals = jnp.einsum("grqk,grqd->kgd", probs.astype(BF), d_attn, preferred_element_type=F32)
    d_kv = jnp.concatenate([d_keys.reshape(4 * rows, kv_width), d_vals.reshape(4 * rows, kv_width)], axis=1)
    (d_kv,) = scatter_call("x", [d_kv.astype(BF).reshape(4, rows, 2 * kv_width)], 4)
    d_q_low = unrotate(d_query.reshape(rows, QH, HD), cosine, sine).reshape(rows, QH * HD).astype(BF)
    d_key = unrotate(d_kv[:, :kv_width].reshape(rows, KVH, HD), cosine, sine).reshape(rows, kv_width)
    d_kv_low = jnp.concatenate([d_key, d_kv[:, kv_width:]], axis=1).astype(BF)
    d_qkv = jnp.concatenate([d_q_low, d_kv_low], axis=1)
    grad_qkv = outer_sum(act_one, d_qkv)
    d_act_one = back_product(d_q_low, wq) + back_product(d_kv_low, wkv)
    d_in_norm, grad_gain_one = pull_one(d_act_one)
    grad_in = (d_mid + d_in_norm).astype(BF)

    qkvo = jnp.concatenate([grad_qkv, grad_o], axis=1).reshape(4, 240, 2560)
    tail = jnp.stack([grad_gain_one, grad_gain_two]).reshape(2, 4, 240).transpose(1, 0, 2)
    tail = jnp.pad(tail, ((0, 0), (0, 14), (0, 2560 - 240)))
    qkvo = jnp.concatenate([qkvo, tail], axis=1).astype(BF)
    gu = jnp.pad(grad_gu.reshape(4, 240, -1), ((0, 0), (0, 16), (0, 0))).astype(BF)
    down_o, gu_o, qkvo_o, hidden_out, grad_in = end_call(
        qkvo, gu, grad_down.astype(BF), result.reshape(2, seg, width), grad_in.reshape(2, seg, width)
    )
    qkvo_o = qkvo_o.astype(F32)
    return (
        hidden_out,
        grad_in,
        qkvo_o[240, :240],
        qkvo_o[241, :240],
        qkvo_o[:240, :960],
        qkvo_o[:240, 960:1600],
        qkvo_o[:240, 1600:],
        gu_o[:240].astype(F32),
        down_o.astype(F32),
    )


def solution(mesh):
    placed = (
        P(None, "wt", "ctx", None),
        P(None, "wt", "ctx", None),
        P(),
        P("wt"),
        P("wt"),
        P("wt", None),
        P("wt", None),
        P("wt", None),
        P("wt", None),
        P("wt", None),
    )
    local = local_fast if dict(mesh.shape) == {"ctx": 8, "wt": 4} else local_general
    return jax.shard_map(
        local,
        mesh=mesh,
        in_specs=placed,
        out_specs=(
            P(None, "wt", "ctx", None),
            P(None, "wt", "ctx", None),
            P("wt"),
            P("wt"),
            P("wt", None),
            P("wt", None),
            P("wt", None),
            P("wt", None),
            P("wt", None),
        ),
        check_vma=False,
    )
```
